256 devices in a mesh: gx: 32 (over y_lo, z, core), gy: 8 (over x, y_hi).
Axes of the slice: x: 4, y: 4 (y_hi: 2, y_lo: 2; y = y_hi * 2 + y_lo), z: 8, core: 2. Of those that a mesh axis runs over, the one named last changes fastest.
Arguments:
- features: bfloat16 [8192, 32, 8, 256], P('gx', 'gy'), may hold values from -6 to 6
- spectral_weight: bfloat16 [16, 2, 256, 256], replicated, may hold values from -6 to 6
- conv_taps: float32 [3, 256], replicated, may hold values from -3 to 3
- w_in: bfloat16 [256, 1024], replicated, may hold values from -0.375 to 0.375
- bias_in: float32 [1024], replicated, may hold values from -3 to 3
- w_out: bfloat16 [1024, 256], replicated, may hold values from -0.1875 to 0.1875
- bias_out: float32 [256], replicated, may hold values from -3 to 3
Outputs:
- layer_out: bfloat16 [8192, 32, 8, 256], P('gx', 'gy')
The draws below stay inside these ranges and needn't reach their ends.
All inputs are finite; a program needn't handle non-finite values.
Results may differ from the reference program's by a relative error of at most 0.0065.
Values may be sent and summed in bfloat16 or wider, within the bound.
A program may use at most 128 MiB of HBM per device.

```python
import math
import jax
import jax.numpy as jnp
from jax import lax

C = 256
HID = 1024
MODES = 16
X = 8192
Z = 8
Y = 32


def block_levels(key, dims, cuts, low, largest):
    gain = 1.0
    for axis_at, shards_of in cuts:
        steps = jax.random.uniform(jax.random.fold_in(jax.random.fold_in(key, 6), axis_at), (shards_of,), jnp.float32, low / len(cuts), largest / len(cuts))
        gain = gain * jnp.repeat(jnp.exp(steps), dims[axis_at] // shards_of).reshape((-1,) + (1,) * (len(dims) - 1 - axis_at))
    return gain


def scatter_about(own_key, dims, spread, limit, cuts=(), held_as=jnp.bfloat16):
    loudness = block_levels(own_key, dims, cuts, -0.22, 0.18) if cuts else 1.0
    array = jax.random.normal(own_key, dims, jnp.float32) * spread * loudness
    return jnp.minimum(jnp.maximum(array, -limit), limit).astype(held_as)


def setup_inputs(seed: int = 0) -> dict:
    streams_of = jax.random.split(jax.random.key(seed), 8)
    return {
        "features": scatter_about(streams_of[0], (X, Y, Z, C), 1.0, 6.0, ((0, 32), (1, 8))),
        "spectral_weight": scatter_about(streams_of[1], (MODES, 2, C, C), 1.0, 6.0),
        "conv_taps": scatter_about(streams_of[2], (3, C), 0.5, 3.0, (), jnp.float32),
        "w_in": scatter_about(streams_of[3], (C, HID), C ** -0.5, 0.375),
        "bias_in": scatter_about(streams_of[4], (HID,), 0.5, 3.0, (), jnp.float32),
        "w_out": scatter_about(streams_of[5], (HID, C), HID ** -0.5, 0.1875),
        "bias_out": scatter_about(streams_of[6], (C,), 0.5, 3.0, (), jnp.float32),
    }


def make_tables(positions, total, mode_count):
    waves = jnp.arange(mode_count, dtype=jnp.int32)
    product = waves[:, None] * positions[None, :] % total
    angles = 2.0 * math.pi / total * product.astype(jnp.float32)
    scale = 1.0 / math.sqrt(total)
    cosines = jnp.cos(angles)
    sines = jnp.sin(angles)
    forward = (jnp.concatenate([cosines, -sines], 0) * scale).astype(jnp.bfloat16)
    amplitude = jnp.where(waves == 0, 1.0, 2.0).astype(jnp.float32)[:, None]
    inverse = (jnp.concatenate([amplitude * cosines, -amplitude * sines], 0) * scale).T.astype(jnp.bfloat16)
    return (forward, inverse)

def reference(features, spectral_weight, conv_taps, w_in, bias_in, w_out, bias_out):
    positions = jnp.arange(X, dtype=jnp.int32)
    forward, inverse = make_tables(positions, X, MODES)
    weight_real = spectral_weight[:, 0].astype(jnp.float32)
    weight_imag = spectral_weight[:, 1].astype(jnp.float32)

    def column(index):
        plane = lax.dynamic_index_in_dim(features, index, 2, keepdims=False)
        flattened = plane.reshape(X, Y * C)
        spectrum = jnp.dot(forward, flattened, preferred_element_type=jnp.float32)
        spectrum_b = spectrum.astype(jnp.bfloat16).astype(jnp.float32).reshape(2, MODES, Y, C)
        mixed_real = jnp.einsum('kyc,kco->kyo', spectrum_b[0], weight_real) - jnp.einsum('kyc,kco->kyo', spectrum_b[1], weight_imag)
        mixed_imag = jnp.einsum('kyc,kco->kyo', spectrum_b[0], weight_imag) + jnp.einsum('kyc,kco->kyo', spectrum_b[1], weight_real)
        mixed = jnp.stack([mixed_real, mixed_imag]).astype(jnp.bfloat16).reshape(2 * MODES, Y * C)
        spectral = jnp.dot(inverse, mixed, preferred_element_type=jnp.float32).reshape(X, Y, C)
        padded = jnp.pad(plane.astype(jnp.float32), ((0, 0), (1, 1), (0, 0)))
        conv = conv_taps[0] * padded[:, :-2] + conv_taps[1] * padded[:, 1:-1] + conv_taps[2] * padded[:, 2:]
        joined = (spectral + conv).astype(jnp.bfloat16).reshape(X * Y, C)
        hidden = jax.nn.gelu(jnp.dot(joined, w_in, preferred_element_type=jnp.float32) + bias_in, approximate=True).astype(jnp.bfloat16)
        result = plane.astype(jnp.float32).reshape(X * Y, C) + jnp.dot(hidden, w_out, preferred_element_type=jnp.float32) + bias_out
        return result.astype(jnp.bfloat16).reshape(X, Y, C)
    stacked = lax.map(column, jnp.arange(Z, dtype=jnp.int32))
    return jnp.transpose(stacked, (1, 2, 0, 3))
```

```python
import functools
import math

import jax
import jax.numpy as jnp
from jax import lax
from jax.experimental import pallas as pl
from jax.experimental.pallas import tpu as pltpu
from jax.sharding import PartitionSpec as P

MESH = pl.DeviceIdType.MESH
BF = jnp.bfloat16
F32 = jnp.float32
X = 8192
MODES = 16
XL = 256
YL = 4
Z = 8
C = 256
HID = 1024
NCH = 16
EARLY = 4
CROWS = XL // NCH
XB = 128
HB = 64
HC = 256


def table(shape, lane_is_mode):
    rows = lax.broadcasted_iota(jnp.int32, shape, 0)
    cols = lax.broadcasted_iota(jnp.int32, shape, 1)
    first = lax.axis_index("gx") * XL
    if lane_is_mode:
        mode, part, x = cols // 16, (cols // 8) % 2, first + rows
    else:
        mode, part, x = rows // 2, rows % 2, first + cols // 8
    turn = (mode * x + part * (X // 4)) % X
    value = jnp.cos((2.0 * math.pi / X) * turn.astype(F32)) * (1.0 / math.sqrt(X))
    if lane_is_mode:
        value = value * jnp.where(mode == 0, 1.0, 2.0)
    return value


def gelu_doubled(x):
    c = math.sqrt(2.0 / math.pi)
    t = jnp.tanh(x * (c + (c * 0.044715) * (x * x)))
    return x + x * t


def kernel(
    f_hbm, sw_hbm, taps_hbm, w1_hbm, b1_hbm, w2_hbm, b2_hbm,
    out,
    fv, fwd, inv, tab, tabt, s32, csend, crecv, zsend, zrecv, ysend, yrecv, wmix, mixed, mg, taps, w1, b1, w2, b2,
    fsem, wsem, hs, hr, cs, cr, zs, zr, ys, yr, gs, gr, ks, kr,
):
    gx, gy = lax.axis_index("gx"), lax.axis_index("gy")
    core = gx % 2
    z = (gx // 2) % 8
    base = gx - 2 * z
    core_peer = (base + 2 * z + 1 - 2 * core, gy)
    y_peer = ((gx + 16) % 32, gy)
    z_index = [(z + d) % 8 for d in range(1, 8)]
    z_peer = [(base + 2 * i, gy) for i in z_index]
    has_next, has_prev = gy < 7, gy > 0
    mode = core * 8 + z

    barrier = pltpu.get_barrier_semaphore()
    for peer in [core_peer, y_peer] + z_peer:
        pl.semaphore_signal(barrier, inc=1, device_id=peer, device_id_type=MESH)

    @pl.when(has_next)
    def _():
        pl.semaphore_signal(barrier, inc=1, device_id=(gx, gy + 1), device_id_type=MESH)

    @pl.when(has_prev)
    def _():
        pl.semaphore_signal(barrier, inc=1, device_id=(gx, gy - 1), device_id_type=MESH)

    loads = [pltpu.make_async_copy(f_hbm.at[:, y], fv.at[y + 1], fsem.at[y]) for y in range(YL)]
    for load in loads:
        load.start()
    others = [
        pltpu.make_async_copy(sw_hbm.at[mode], wmix, wsem.at[0]),
        pltpu.make_async_copy(w1_hbm, w1, wsem.at[1]),
        pltpu.make_async_copy(w2_hbm, w2, wsem.at[2]),
        pltpu.make_async_copy(b1_hbm, b1, wsem.at[3]),
        pltpu.make_async_copy(b2_hbm, b2, wsem.at[4]),
        pltpu.make_async_copy(taps_hbm, taps, wsem.at[5]),
    ]
    for load in others:
        load.start()

    tab[...] = table((2 * MODES, XL * Z), False)
    lane = lax.broadcasted_iota(jnp.int32, (8, XL * Z), 1) % 8
    own = (lane == lax.broadcasted_iota(jnp.int32, (8, XL * Z), 0)).astype(F32)
    for i in range(MODES):
        pair = [own * tab[2 * i + p : 2 * i + p + 1, :] for p in range(2)]
        fwd[16 * i : 16 * i + 16, :] = jnp.concatenate(pair, 0).astype(BF)

    for y in range(YL):
        loads[y].wait()
        s = jnp.dot(fwd[...], fv[y + 1].reshape(XL * Z, C), preferred_element_type=F32)
        s32[:, y] = s.reshape(MODES, 16, C)
    for k in range(8):
        csend[k] = s32[(1 - core) * 8 + k].astype(BF)

    pl.semaphore_wait(barrier, 9 + has_next.astype(jnp.int32) + has_prev.astype(jnp.int32))

    def to_next(c):
        rows = pl.ds(c * CROWS, CROWS)
        return pltpu.make_async_remote_copy(
            f_hbm.at[rows, YL - 1], fv.at[0, rows], hs.at[0, c], hr.at[0, c],
            device_id=(gx, gy + 1), device_id_type=MESH,
        )

    def to_prev(c):
        rows = pl.ds(c * CROWS, CROWS)
        return pltpu.make_async_remote_copy(
            f_hbm.at[rows, 0], fv.at[YL + 1, rows], hs.at[1, c], hr.at[1, c],
            device_id=(gx, gy - 1), device_id_type=MESH,
        )

    def send_halo(first, last):
        @pl.loop(first, last)
        def _(c):
            @pl.when(has_next)
            def _():
                to_next(c).start()

            @pl.when(has_prev)
            def _():
                to_prev(c).start()

    to_core = pltpu.make_async_remote_copy(csend, crecv, cs, cr, device_id=core_peer, device_id_type=MESH)
    to_core.start()
    send_halo(0, EARLY)
    to_core.wait()

    to_z = []
    for d in range(7):
        zo = z_index[d]
        zsend[d] = (s32[core * 8 + zo] + crecv[zo].astype(F32)).astype(BF)
        copy = pltpu.make_async_remote_copy(
            zsend.at[d], zrecv.at[d], zs.at[d], zr.at[d], device_id=z_peer[d], device_id_type=MESH
        )
        copy.start()
        to_z.append(copy)
    total = s32[mode] + crecv[z].astype(F32)

    tabt[...] = table((XL, C), True)
    lane = lax.broadcasted_iota(jnp.int32, (8, C), 1) % 8
    own = (lane == lax.broadcasted_iota(jnp.int32, (8, C), 0)).astype(F32)

    @pl.loop(0, XL // 8)
    def _(i):
        rows = tabt[pl.ds(pl.multiple_of(i * 8, 8), 8), :]
        spread = [own * rows[r : r + 1, :] for r in range(8)]
        inv[pl.ds(pl.multiple_of(i * 64, 64), 64), :] = jnp.concatenate(spread, 0).astype(BF)

    @pl.when(jnp.logical_not(has_prev))
    def _():
        fv[0] = jnp.zeros((XL, Z, C), BF)

    @pl.when(jnp.logical_not(has_next))
    def _():
        fv[YL + 1] = jnp.zeros((XL, Z, C), BF)

    for load in others:
        load.wait()
    for copy in to_z:
        copy.wait()
    for d in range(7):
        total = total + zrecv[d].astype(F32)

    ysend[...] = total.astype(BF)
    to_y = pltpu.make_async_remote_copy(ysend, yrecv, ys, yr, device_id=y_peer, device_id_type=MESH)
    to_y.start()
    send_halo(EARLY, NCH)
    to_y.wait()
    total = ysend[...].astype(F32) + yrecv[...].astype(F32)

    real = total[:, 0:8].reshape(YL * Z, C)
    imag = total[:, 8:16].reshape(YL * Z, C)
    both = jnp.concatenate([real, imag], 0).astype(BF)
    by_real = jnp.dot(both, wmix[0], preferred_element_type=F32)
    by_imag = jnp.dot(both, wmix[1], preferred_element_type=F32)
    n = YL * Z
    mixed_real = (by_real[:n] - by_imag[n:]).reshape(YL, 8, C)
    mixed_imag = (by_imag[:n] + by_real[n:]).reshape(YL, 8, C)
    result = jnp.concatenate([mixed_real, mixed_imag], 1).astype(BF)
    mixed[...] = result
    mg[:, mode] = result

    def to_all(d):
        return pltpu.make_async_remote_copy(
            mixed, mg.at[:, mode], gs.at[d], gr.at[d], device_id=z_peer[d], device_id_type=MESH
        )

    def from_z(d):
        zo = (z + 7 - d) % 8
        return pltpu.make_async_remote_copy(
            mixed, mg.at[:, core * 8 + zo], gs.at[d], gr.at[d], device_id=z_peer[d], device_id_type=MESH
        )

    def forward(src, slot, i):
        return pltpu.make_async_remote_copy(
            src, mg.at[:, slot], ks.at[i], kr.at[i], device_id=core_peer, device_id_type=MESH
        )

    order = [3, 2, 4, 1, 5, 0, 6]
    arrive = [0, 6, 1, 5, 2, 4, 3]
    for d in order:
        to_all(d).start()
    first = forward(mixed, mode, 7)
    first.start()
    relays = [first]
    for d in arrive:
        from_z(d).wait_recv()
        slot = core * 8 + (z + 7 - d) % 8
        relay = forward(mg.at[:, slot], slot, d)
        relay.start()
        relays.append(relay)
    for d in order:
        to_all(d).wait_send()
    for relay in relays:
        relay.wait()

    def mlp(joined, center):
        acc = center + b2[...]
        for h in range(0, HID, HC):
            hidden = jnp.dot(joined, w1[:, h : h + HC], preferred_element_type=F32) + b1[:, h : h + HC]
            hidden = gelu_doubled(hidden).astype(BF)
            acc = acc + 0.5 * jnp.dot(hidden, w2[h : h + HC, :], preferred_element_type=F32)
        return acc

    def joined_of(y, x0, cells):
        n = cells * Z
        rows = pl.ds(pl.multiple_of(x0 * Z, n), n)
        at = pl.ds(x0, cells)
        value = jnp.dot(inv[rows, :], mg[y].reshape(C, C), preferred_element_type=F32)
        near = [fv[y + i, at].reshape(n, C).astype(F32) for i in range(3)]
        conv = taps[0:1] * near[0] + taps[1:2] * near[1] + taps[2:3] * near[2]
        return (value + conv).astype(BF), near[1]

    per_row = XL // XB

    @pl.loop(0, 2 * per_row)
    def _(i):
        y = 1 + i // per_row
        x0 = pl.multiple_of((i % per_row) * XB, XB)
        joined, center = joined_of(y, x0, XB)
        out[pl.ds(x0, XB), y] = mlp(joined, center).astype(BF).reshape(XB, Z, C)

    per_block = HB // CROWS

    @pl.loop(0, XL // HB)
    def _(i):
        x0 = pl.multiple_of(i * HB, HB)

        @pl.loop(i * per_block, (i + 1) * per_block)
        def _(c):
            @pl.when(has_next)
            def _():
                to_next(c).wait_send()
                to_prev(c).wait_recv()

            @pl.when(has_prev)
            def _():
                to_prev(c).wait_send()
                to_next(c).wait_recv()

        low, low_center = joined_of(0, x0, HB)
        high, high_center = joined_of(YL - 1, x0, HB)
        value = mlp(jnp.concatenate([low, high], 0), jnp.concatenate([low_center, high_center], 0))
        value = value.astype(BF)
        out[pl.ds(x0, HB), 0] = value[: HB * Z].reshape(HB, Z, C)
        out[pl.ds(x0, HB), YL - 1] = value[HB * Z :].reshape(HB, Z, C)


def local(features, spectral_weight, conv_taps, w_in, bias_in, w_out, bias_out):
    dma = pltpu.SemaphoreType.DMA
    vm = pltpu.VMEM
    return pl.pallas_call(
        kernel,
        out_shape=jax.ShapeDtypeStruct((XL, YL, Z, C), BF),
        in_specs=[pl.BlockSpec(memory_space=pl.ANY)] * 7,
        out_specs=pl.BlockSpec(memory_space=pltpu.VMEM),
        scratch_shapes=[
            vm((YL + 2, XL, Z, C), BF),
            vm((2 * MODES * 8, XL * Z), BF),
            vm((XL * Z, C), BF),
            vm((2 * MODES, XL * Z), F32),
            vm((XL, C), F32),
            vm((MODES, YL, 16, C), F32),
            vm((8, YL, 16, C), BF),
            vm((8, YL, 16, C), BF),
            vm((7, YL, 16, C), BF),
            vm((7, YL, 16, C), BF),
            vm((YL, 16, C), BF),
            vm((YL, 16, C), BF),
            vm((2, C, C), BF),
            vm((YL, 16, C), BF),
            vm((YL, MODES, 16, C), BF),
            vm((3, C), F32),
            vm((C, HID), BF),
            vm((1, HID), F32),
            vm((HID, C), BF),
            vm((1, C), F32),
            dma((YL,)),
            dma((6,)),
            dma((2, NCH)),
            dma((2, NCH)),
            dma,
            dma,
            dma((7,)),
            dma((7,)),
            dma,
            dma,
            dma((7,)),
            dma((7,)),
            dma((8,)),
            dma((8,)),
        ],
        compiler_params=pltpu.CompilerParams(
            collective_id=0, has_side_effects=True, vmem_limit_bytes=56 << 20
        ),
        name="layer",
    )(
        features,
        spectral_weight,
        conv_taps,
        w_in,
        bias_in.reshape(1, HID),
        w_out,
        bias_out.reshape(1, C),
    )


def solution(mesh):
    return jax.shard_map(
        local,
        mesh=mesh,
        in_specs=(P("gx", "gy", None, None), P(), P(), P(), P(), P(), P()),
        out_specs=P("gx", "gy", None, None),
        check_vma=False,
    )
```

```python
import functools
import math

import jax
import jax.numpy as jnp
from jax import lax
from jax.experimental import pallas as pl
from jax.experimental.pallas import tpu as pltpu
from jax.sharding import PartitionSpec as P

MESH = pl.DeviceIdType.MESH
BF = jnp.bfloat16
F32 = jnp.float32
X = 8192
MODES = 16
XL = 256
YL = 4
Z = 8
C = 256
HID = 1024
NCH = 16
EARLY = 5
CROWS = XL // NCH
XB = 128
HB = 64
RELAY = 12
LAST = XL - HB
HC = 256


def table(shape, lane_is_mode):
    rows = lax.broadcasted_iota(jnp.int32, shape, 0)
    cols = lax.broadcasted_iota(jnp.int32, shape, 1)
    first = lax.axis_index("gx") * XL
    if lane_is_mode:
        mode, part, x = cols // 16, (cols // 8) % 2, first + rows
    else:
        mode, part, x = rows // 2, rows % 2, first + cols // 8
    turn = (mode * x + part * (X // 4)) % X
    value = jnp.cos((2.0 * math.pi / X) * turn.astype(F32)) * (1.0 / math.sqrt(X))
    if lane_is_mode:
        value = value * jnp.where(mode == 0, 1.0, 2.0)
    return value


def gelu_doubled(x):
    c = math.sqrt(2.0 / math.pi)
    t = jnp.tanh(x * (c + (c * 0.044715) * (x * x)))
    return x + x * t


def mlp(joined, center, w1, b1, w2, b2):
    acc = None
    for h in range(0, HID, HC):
        hidden = jnp.dot(joined, w1[:, h : h + HC], preferred_element_type=F32) + b1[:, h : h + HC]
        hidden = gelu_doubled(hidden).astype(BF)
        part = jnp.dot(hidden, w2[h : h + HC, :], preferred_element_type=F32)
        acc = part if acc is None else acc + part
    return center + b2[...] + 0.5 * acc


def kernel(
    f_hbm, sw_hbm, taps_hbm, w1_hbm, b1_hbm, w2_hbm, b2_hbm,
    out, last,
    ov, jv, rl, fv, fwd, inv, tab, tabt, s32, csend, crecv, zsend, zrecv, ysend, yrecv, wmix, mixed, mg, taps, w1, b1, w2, b2,
    fsem, wsem, hs, hr, cs, cr, zs, zr, ys, yr, gs, gr, ks, kr, rr, fs, osem,
):
    gx, gy = lax.axis_index("gx"), lax.axis_index("gy")
    core = gx % 2
    z = (gx // 2) % 8
    base = gx - 2 * z
    core_peer = (base + 2 * z + 1 - 2 * core, gy)
    y_peer = ((gx + 16) % 32, gy)
    z_index = [(z + d) % 8 for d in range(1, 8)]
    z_peer = [(base + 2 * i, gy) for i in z_index]
    mode = core * 8 + z
    column, high = gy // 2, gy % 2
    same = gy + 1 - 2 * high
    diff = gy - 1 + 2 * high
    has_next, has_prev = gy < 7, gy > 0
    has_diff = (diff >= 0) & (diff <= 7)
    from_low, from_high = gy > 1, gy < 6
    relay_to = jnp.where(high == 0, gy + 2, gy - 2)
    sent_by_relay = jnp.where(high == 1, 12 - 4 * column, 4 * column)
    passed_on = jnp.where(high == 0, 12 - 4 * column, 4 * column)

    barrier = pltpu.get_barrier_semaphore()
    for peer in [core_peer, y_peer, (gx, same)] + z_peer:
        pl.semaphore_signal(barrier, inc=1, device_id=peer, device_id_type=MESH)
    for there, peer in ((has_diff, diff), (from_low, gy - 2), (from_high, gy + 2)):

        @pl.when(there)
        def _():
            pl.semaphore_signal(barrier, inc=1, device_id=(gx, peer), device_id_type=MESH)

    loads = [pltpu.make_async_copy(f_hbm.at[:, y], fv.at[y + 1], fsem.at[y]) for y in range(YL)]
    for load in loads:
        load.start()
    others = [
        pltpu.make_async_copy(sw_hbm.at[mode], wmix, wsem.at[0]),
        pltpu.make_async_copy(w1_hbm, w1, wsem.at[1]),
        pltpu.make_async_copy(w2_hbm, w2, wsem.at[2]),
        pltpu.make_async_copy(b1_hbm, b1, wsem.at[3]),
        pltpu.make_async_copy(b2_hbm, b2, wsem.at[4]),
        pltpu.make_async_copy(taps_hbm, taps, wsem.at[5]),
    ]
    for load in others:
        load.start()

    tab[...] = table((2 * MODES, XL * Z), False)
    lane = lax.broadcasted_iota(jnp.int32, (8, XL * Z), 1) % 8
    own = (lane == lax.broadcasted_iota(jnp.int32, (8, XL * Z), 0)).astype(F32)
    for i in range(MODES):
        pair = [own * tab[2 * i + p : 2 * i + p + 1, :] for p in range(2)]
        fwd[16 * i : 16 * i + 16, :] = jnp.concatenate(pair, 0).astype(BF)

    for y in range(YL):
        loads[y].wait()
        s = jnp.dot(fwd[...], fv[y + 1].reshape(XL * Z, C), preferred_element_type=F32)
        s32[:, y] = s.reshape(MODES, 16, C)
    for k in range(8):
        csend[k] = s32[(1 - core) * 8 + k].astype(BF)

    pl.semaphore_wait(barrier, 10 + sum(there.astype(jnp.int32) for there in (has_diff, from_low, from_high)))

    row_same, slot_same = jnp.where(high == 0, YL - 1, 0), jnp.where(high == 0, 0, YL + 1)
    row_diff, slot_diff = jnp.where(high == 1, YL - 1, 0), jnp.where(high == 1, 0, YL + 1)

    def send_same(c):
        rows = pl.ds(c * CROWS, CROWS)
        return pltpu.make_async_remote_copy(
            f_hbm.at[rows, row_same], fv.at[slot_same, rows], hs.at[0, c], hr.at[0, c],
            device_id=(gx, same), device_id_type=MESH,
        )

    def send_diff(c):
        rows = pl.ds(c * CROWS, CROWS)
        return pltpu.make_async_remote_copy(
            f_hbm.at[rows, row_diff], fv.at[slot_diff, rows], hs.at[1, c], hr.at[1, c],
            device_id=(gx, diff), device_id_type=MESH,
        )

    def send_relay(c):
        rows = pl.ds(c * CROWS, CROWS)
        return pltpu.make_async_remote_copy(
            f_hbm.at[rows, row_diff], rl.at[c], hs.at[1, c], rr.at[c],
            device_id=(gx, same), device_id_type=MESH,
        )

    def pass_on(c):
        rows = pl.ds(c * CROWS, CROWS)
        return pltpu.make_async_remote_copy(
            rl.at[c], fv.at[slot_same, rows], fs.at[c], hr.at[1, c],
            device_id=(gx, relay_to), device_id_type=MESH,
        )

    def send_halo(first, last):
        @pl.loop(first, last)
        def _(c):
            send_same(c).start()

            @pl.when(has_diff & (c < sent_by_relay))
            def _():
                send_relay(c).start()

            @pl.when(has_diff & (c >= sent_by_relay))
            def _():
                send_diff(c).start()

    def relay_halo(first, last):
        @pl.loop(first, last)
        def _(c):
            @pl.when(c < passed_on)
            def _():
                send_relay(c).wait_recv()
                pass_on(c).start()

    to_core = pltpu.make_async_remote_copy(csend, crecv, cs, cr, device_id=core_peer, device_id_type=MESH)
    to_core.start()
    send_halo(0, EARLY)
    to_core.wait()

    to_z = []
    order = [3, 2, 4, 1, 5, 0, 6]
    for d in order:
        zo = z_index[d]
        zsend[d] = (s32[core * 8 + zo] + crecv[zo].astype(F32)).astype(BF)
        copy = pltpu.make_async_remote_copy(
            zsend.at[d], zrecv.at[d], zs.at[d], zr.at[d], device_id=z_peer[d], device_id_type=MESH
        )
        copy.start()
        to_z.append(copy)
    total = s32[mode] + crecv[z].astype(F32)

    tabt[...] = table((XL, C), True)
    lane = lax.broadcasted_iota(jnp.int32, (8, C), 1) % 8
    own = (lane == lax.broadcasted_iota(jnp.int32, (8, C), 0)).astype(F32)

    @pl.loop(0, XL // 8)
    def _(i):
        rows = tabt[pl.ds(pl.multiple_of(i * 8, 8), 8), :]
        spread = [own * rows[r : r + 1, :] for r in range(8)]
        inv[pl.ds(pl.multiple_of(i * 64, 64), 64), :] = jnp.concatenate(spread, 0).astype(BF)

    @pl.when(jnp.logical_not(has_prev))
    def _():
        fv[0] = jnp.zeros((XL, Z, C), BF)

    @pl.when(jnp.logical_not(has_next))
    def _():
        fv[YL + 1] = jnp.zeros((XL, Z, C), BF)

    for load in others:
        load.wait()
    for copy in to_z:
        copy.wait()
    for d in range(7):
        total = total + zrecv[d].astype(F32)

    ysend[...] = total.astype(BF)
    to_y = pltpu.make_async_remote_copy(ysend, yrecv, ys, yr, device_id=y_peer, device_id_type=MESH)
    to_y.start()
    send_halo(EARLY, NCH)
    to_y.wait()
    total = ysend[...].astype(F32) + yrecv[...].astype(F32)

    real = total[:, 0:8].reshape(YL * Z, C)
    imag = total[:, 8:16].reshape(YL * Z, C)
    both = jnp.concatenate([real, imag], 0).astype(BF)
    by_real = jnp.dot(both, wmix[0], preferred_element_type=F32)
    by_imag = jnp.dot(both, wmix[1], preferred_element_type=F32)
    n = YL * Z
    mixed_real = (by_real[:n] - by_imag[n:]).reshape(YL, 8, C)
    mixed_imag = (by_imag[:n] + by_real[n:]).reshape(YL, 8, C)
    result = jnp.concatenate([mixed_real, mixed_imag], 1).astype(BF)
    mixed[...] = result
    mg[:, mode] = result

    def to_all(d):
        return pltpu.make_async_remote_copy(
            mixed, mg.at[:, mode], gs.at[d], gr.at[d], device_id=z_peer[d], device_id_type=MESH
        )

    def from_z(d):
        zo = (z + 7 - d) % 8
        return pltpu.make_async_remote_copy(
            mixed, mg.at[:, core * 8 + zo], gs.at[d], gr.at[d], device_id=z_peer[d], device_id_type=MESH
        )

    def forward(src, slot, i):
        return pltpu.make_async_remote_copy(
            src, mg.at[:, slot], ks.at[i], kr.at[i], device_id=core_peer, device_id_type=MESH
        )

    arrive = [0, 6, 1, 5, 2, 4, 3]
    for d in order:
        to_all(d).start()
    relay_halo(0, 4)
    first = forward(mixed, mode, 7)
    first.start()
    relays = [first]
    for d in arrive:
        from_z(d).wait_recv()
        slot = core * 8 + (z + 7 - d) % 8
        relay = forward(mg.at[:, slot], slot, d)
        relay.start()
        relays.append(relay)
    for d in order:
        to_all(d).wait_send()
    for relay in relays:
        relay.wait()

    relay_halo(4, 8)

    def joined_of(y, x0, cells):
        n = cells * Z
        rows = pl.ds(pl.multiple_of(x0 * Z, n), n)
        at = pl.ds(x0, cells)
        value = jnp.dot(inv[rows, :], mg[y].reshape(C, C), preferred_element_type=F32)
        near = [fv[y + i, at].reshape(n, C).astype(F32) for i in range(3)]
        conv = taps[0:1] * near[0] + taps[1:2] * near[1] + taps[2:3] * near[2]
        return (value + conv).astype(BF), near[1]

    per_row = XL // XB

    @pl.loop(0, 2 * per_row)
    def _(i):
        y = 1 + i // per_row
        x0 = pl.multiple_of((i % per_row) * XB, XB)
        joined, center = joined_of(y, x0, XB)
        ov[pl.ds(x0, XB), y] = mlp(joined, center, w1, b1, w2, b2).astype(BF).reshape(XB, Z, C)

    inner = pltpu.make_async_copy(ov.at[:, 1:3], out.at[:, 1:3], osem.at[0])
    inner.start()
    relay_halo(8, RELAY)

    per_block = HB // CROWS

    def outer(i):
        x0 = pl.multiple_of(i * HB, HB)

        @pl.loop(i * per_block, (i + 1) * per_block)
        def _(c):
            send_same(c).wait()

            @pl.when(has_diff)
            def _():
                send_diff(c).wait()

        low, low_center = joined_of(0, x0, HB)
        high_, high_center = joined_of(YL - 1, x0, HB)
        return jnp.concatenate([low, high_], 0), jnp.concatenate([low_center, high_center], 0)

    def store(i, row, k):
        rows = pl.ds(i * HB, HB)
        return pltpu.make_async_copy(ov.at[rows, row], out.at[rows, row], osem.at[k])

    @pl.loop(0, LAST // HB)
    def _(i):
        joined, center = outer(i)
        value = mlp(joined, center, w1, b1, w2, b2).astype(BF)
        rows = pl.ds(i * HB, HB)
        ov[rows, 0] = value[: HB * Z].reshape(HB, Z, C)
        ov[rows, YL - 1] = value[HB * Z :].reshape(HB, Z, C)
        store(i, 0, 1 + 2 * i).start()
        store(i, YL - 1, 2 + 2 * i).start()

    jv[...] = outer(LAST // HB)[0]
    final = pltpu.make_async_copy(jv, last, osem.at[7])
    final.start()

    @pl.loop(0, RELAY)
    def _(c):
        @pl.when(c < passed_on)
        def _():
            pass_on(c).wait_send()

    inner.wait()
    for i in range(LAST // HB):
        store(i, 0, 1 + 2 * i).wait()
        store(i, YL - 1, 2 + 2 * i).wait()
    final.wait()


def tail(part, f_hbm, joined_hbm, w1, b1, w2, b2, out, ov, fv, jv, isem, osem, jsem, fsem):
    get_joined = pltpu.make_async_copy(joined_hbm, jv, jsem)
    get_joined.start()
    centers = [pltpu.make_async_copy(f_hbm.at[LAST:, (YL - 1) * i], fv.at[i], fsem.at[i]) for i in range(2)]
    for copy in centers:
        copy.start()
    n = XL // HB
    pieces = [slice(i * HB, (i + 1) * HB) for i in range(n)]
    get = [pltpu.make_async_copy(part.at[p], ov.at[p], isem.at[i]) for i, p in enumerate(pieces[:-1])]
    get.append(pltpu.make_async_copy(part.at[LAST:, 1:3], ov.at[LAST:, 1:3], isem.at[n - 1]))
    put = [pltpu.make_async_copy(ov.at[p], out.at[p], osem.at[i]) for i, p in enumerate(pieces)]
    for copy in get:
        copy.start()
    for i in range(n - 1):
        get[i].wait()
        put[i].start()
    get_joined.wait()
    for copy in centers:
        copy.wait()
    value = mlp(jv[...], fv[...].reshape(2 * HB * Z, C).astype(F32), w1, b1, w2, b2).astype(BF)
    get[n - 1].wait()
    ov[LAST:, 0] = value[: HB * Z].reshape(HB, Z, C)
    ov[LAST:, YL - 1] = value[HB * Z :].reshape(HB, Z, C)
    put[n - 1].start()
    for copy in put:
        copy.wait()


def local(features, spectral_weight, conv_taps, w_in, bias_in, w_out, bias_out):
    dma = pltpu.SemaphoreType.DMA
    vm = pltpu.VMEM
    b1, b2 = bias_in.reshape(1, HID), bias_out.reshape(1, C)
    part, last = pl.pallas_call(
        kernel,
        out_shape=[jax.ShapeDtypeStruct((XL, YL, Z, C), BF), jax.ShapeDtypeStruct((2 * HB * Z, C), BF)],
        in_specs=[pl.BlockSpec(memory_space=pltpu.HBM)] * 7,
        out_specs=[pl.BlockSpec(memory_space=pl.ANY)] * 2,
        scratch_shapes=[
            vm((XL, YL, Z, C), BF),
            vm((2 * HB * Z, C), BF),
            vm((RELAY, CROWS, Z, C), BF),
            vm((YL + 2, XL, Z, C), BF),
            vm((2 * MODES * 8, XL * Z), BF),
            vm((XL * Z, C), BF),
            vm((2 * MODES, XL * Z), F32),
            vm((XL, C), F32),
            vm((MODES, YL, 16, C), F32),
            vm((8, YL, 16, C), BF),
            vm((8, YL, 16, C), BF),
            vm((7, YL, 16, C), BF),
            vm((7, YL, 16, C), BF),
            vm((YL, 16, C), BF),
            vm((YL, 16, C), BF),
            vm((2, C, C), BF),
            vm((YL, 16, C), BF),
            vm((YL, MODES, 16, C), BF),
            vm((3, C), F32),
            vm((C, HID), BF),
            vm((1, HID), F32),
            vm((HID, C), BF),
            vm((1, C), F32),
            dma((YL,)),
            dma((6,)),
            dma((2, NCH)),
            dma((2, NCH)),
            dma,
            dma,
            dma((7,)),
            dma((7,)),
            dma,
            dma,
            dma((7,)),
            dma((7,)),
            dma((8,)),
            dma((8,)),
            dma((RELAY,)),
            dma((RELAY,)),
            dma((8,)),
        ],
        compiler_params=pltpu.CompilerParams(
            collective_id=0, has_side_effects=True, vmem_limit_bytes=36 << 20
        ),
        name="layer",
    )(*[pltpu.with_memory_space_constraint(a, pltpu.HBM) for a in (features, spectral_weight, conv_taps, w_in, b1, w_out, b2)])
    whole = pl.BlockSpec(memory_space=pltpu.VMEM)
    hbm = pl.BlockSpec(memory_space=pl.ANY)
    return pl.pallas_call(
        tail,
        out_shape=jax.ShapeDtypeStruct((XL, YL, Z, C), BF),
        in_specs=[hbm, pl.BlockSpec(memory_space=pltpu.HBM), hbm] + [whole] * 4,
        out_specs=hbm,
        scratch_shapes=[
            vm((XL, YL, Z, C), BF),
            vm((2, HB, Z, C), BF),
            vm((2 * HB * Z, C), BF),
            dma((XL // HB,)),
            dma((XL // HB,)),
            dma,
            dma((2,)),
        ],
        compiler_params=pltpu.CompilerParams(vmem_limit_bytes=24 << 20),
        name="tail",
    )(part, pltpu.with_memory_space_constraint(features, pltpu.HBM), last, w_in, b1, w_out, b2)


def solution(mesh):
    return jax.shard_map(
        local,
        mesh=mesh,
        in_specs=(P("gx", "gy", None, None), P(), P(), P(), P(), P(), P()),
        out_specs=P("gx", "gy", None, None),
        check_vma=False,
    )
```

```python
import functools
import math

import jax
import jax.numpy as jnp
from jax import lax
from jax.experimental import pallas as pl
from jax.experimental.pallas import tpu as pltpu
from jax.sharding import PartitionSpec as P

MESH = pl.DeviceIdType.MESH
BF = jnp.bfloat16
F32 = jnp.float32
X = 8192
MODES = 16
XL = 256
YL = 4
Z = 8
C = 256
HID = 1024
NCH = 16
EARLY = 5
CROWS = XL // NCH
XB = 128
HB = 64
RELAY = 12
TB = 32
LAST = XL - TB
HC = 256


def table(shape, lane_is_mode):
    rows = lax.broadcasted_iota(jnp.int32, shape, 0)
    cols = lax.broadcasted_iota(jnp.int32, shape, 1)
    first = lax.axis_index("gx") * XL
    if lane_is_mode:
        mode, part, x = cols // 16, (cols // 8) % 2, first + rows
    else:
        mode, part, x = rows // 2, rows % 2, first + cols // 8
    turn = (mode * x + part * (X // 4)) % X
    value = jnp.cos((2.0 * math.pi / X) * turn.astype(F32)) * (1.0 / math.sqrt(X))
    if lane_is_mode:
        value = value * jnp.where(mode == 0, 1.0, 2.0)
    return value


def gelu_doubled(x):
    c = math.sqrt(2.0 / math.pi)
    t = jnp.tanh(x * (c + (c * 0.044715) * (x * x)))
    return x + x * t


def mlp(joined, center, w1, b1, w2, b2):
    acc = None
    for h in range(0, HID, HC):
        hidden = jnp.dot(joined, w1[:, h : h + HC], preferred_element_type=F32) + b1[:, h : h + HC]
        hidden = gelu_doubled(hidden).astype(BF)
        part = jnp.dot(hidden, w2[h : h + HC, :], preferred_element_type=F32)
        acc = part if acc is None else acc + part
    return center + b2[...] + 0.5 * acc


def kernel(
    f_hbm, sw_hbm, taps_hbm, w1_hbm, b1_hbm, w2_hbm, b2_hbm,
    out, last,
    ov, jv, rl, fv, fwd, inv, tab, tabt, s32, csend, crecv, zsend, zrecv, ysend, yrecv, wmix, mixed, mg, taps, w1, b1, w2, b2,
    fsem, wsem, hs, hr, cs, cr, zs, zr, ys, yr, gs, gr, ks, kr, rr, fs, osem,
):
    gx, gy = lax.axis_index("gx"), lax.axis_index("gy")
    core = gx % 2
    z = (gx // 2) % 8
    base = gx - 2 * z
    core_peer = (base + 2 * z + 1 - 2 * core, gy)
    y_peer = ((gx + 16) % 32, gy)
    z_index = [(z + d) % 8 for d in range(1, 8)]
    z_peer = [(base + 2 * i, gy) for i in z_index]
    mode = core * 8 + z
    column, high = gy // 2, gy % 2
    same = gy + 1 - 2 * high
    diff = gy - 1 + 2 * high
    has_next, has_prev = gy < 7, gy > 0
    has_diff = (diff >= 0) & (diff <= 7)
    from_low, from_high = gy > 1, gy < 6
    relay_to = jnp.where(high == 0, gy + 2, gy - 2)
    sent_by_relay = jnp.where(high == 1, 12 - 4 * column, 4 * column)
    passed_on = jnp.where(high == 0, 12 - 4 * column, 4 * column)

    barrier = pltpu.get_barrier_semaphore()
    for peer in [core_peer, y_peer, (gx, same)] + z_peer:
        pl.semaphore_signal(barrier, inc=1, device_id=peer, device_id_type=MESH)
    for there, peer in ((has_diff, diff), (from_low, gy - 2), (from_high, gy + 2)):

        @pl.when(there)
        def _():
            pl.semaphore_signal(barrier, inc=1, device_id=(gx, peer), device_id_type=MESH)

    loads = [pltpu.make_async_copy(f_hbm.at[:, y], fv.at[y + 1], fsem.at[y]) for y in range(YL)]
    for load in loads:
        load.start()
    others = [
        pltpu.make_async_copy(sw_hbm.at[mode], wmix, wsem.at[0]),
        pltpu.make_async_copy(w1_hbm, w1, wsem.at[1]),
        pltpu.make_async_copy(w2_hbm, w2, wsem.at[2]),
        pltpu.make_async_copy(b1_hbm, b1, wsem.at[3]),
        pltpu.make_async_copy(b2_hbm, b2, wsem.at[4]),
        pltpu.make_async_copy(taps_hbm, taps, wsem.at[5]),
    ]
    for load in others:
        load.start()

    tab[...] = table((2 * MODES, XL * Z), False)
    lane = lax.broadcasted_iota(jnp.int32, (8, XL * Z), 1) % 8
    own = (lane == lax.broadcasted_iota(jnp.int32, (8, XL * Z), 0)).astype(F32)
    for i in range(MODES):
        pair = [own * tab[2 * i + p : 2 * i + p + 1, :] for p in range(2)]
        fwd[16 * i : 16 * i + 16, :] = jnp.concatenate(pair, 0).astype(BF)

    for y in range(YL):
        loads[y].wait()
        s = jnp.dot(fwd[...], fv[y + 1].reshape(XL * Z, C), preferred_element_type=F32)
        s32[:, y] = s.reshape(MODES, 16, C)
    for k in range(8):
        csend[k] = s32[(1 - core) * 8 + k].astype(BF)

    pl.semaphore_wait(barrier, 10 + sum(there.astype(jnp.int32) for there in (has_diff, from_low, from_high)))

    row_same, slot_same = jnp.where(high == 0, YL - 1, 0), jnp.where(high == 0, 0, YL + 1)
    row_diff, slot_diff = jnp.where(high == 1, YL - 1, 0), jnp.where(high == 1, 0, YL + 1)

    def send_same(c):
        rows = pl.ds(c * CROWS, CROWS)
        return pltpu.make_async_remote_copy(
            f_hbm.at[rows, row_same], fv.at[slot_same, rows], hs.at[0, c], hr.at[0, c],
            device_id=(gx, same), device_id_type=MESH,
        )

    def send_diff(c):
        rows = pl.ds(c * CROWS, CROWS)
        return pltpu.make_async_remote_copy(
            f_hbm.at[rows, row_diff], fv.at[slot_diff, rows], hs.at[1, c], hr.at[1, c],
            device_id=(gx, diff), device_id_type=MESH,
        )

    def send_relay(c):
        rows = pl.ds(c * CROWS, CROWS)
        return pltpu.make_async_remote_copy(
            f_hbm.at[rows, row_diff], rl.at[c], hs.at[1, c], rr.at[c],
            device_id=(gx, same), device_id_type=MESH,
        )

    def pass_on(c):
        rows = pl.ds(c * CROWS, CROWS)
        return pltpu.make_async_remote_copy(
            rl.at[c], fv.at[slot_same, rows], fs.at[c], hr.at[1, c],
            device_id=(gx, relay_to), device_id_type=MESH,
        )

    def start_diff(c):
        @pl.when(has_diff & (c < sent_by_relay))
        def _():
            send_relay(c).start()

        @pl.when(has_diff & (c >= sent_by_relay))
        def _():
            send_diff(c).start()

    def send_halo(first, last):
        @pl.loop(first, last)
        def _(c):
            send_same(c).start()

            @pl.when(c < 12)
            def _():
                start_diff(c + c // 3)

            @pl.when((c < 12) & (c % 3 == 2))
            def _():
                start_diff(c + c // 3 + 1)

    def relay_halo(first, last):
        @pl.loop(first, last)
        def _(c):
            @pl.when(c < passed_on)
            def _():
                send_relay(c).wait_recv()
                pass_on(c).start()

    to_core = pltpu.make_async_remote_copy(csend, crecv, cs, cr, device_id=core_peer, device_id_type=MESH)
    to_core.start()
    send_halo(0, EARLY)
    to_core.wait()

    to_z = []
    order = [3, 2, 4, 1, 5, 0, 6]
    for d in order:
        zo = z_index[d]
        zsend[d] = (s32[core * 8 + zo] + crecv[zo].astype(F32)).astype(BF)
        copy = pltpu.make_async_remote_copy(
            zsend.at[d], zrecv.at[d], zs.at[d], zr.at[d], device_id=z_peer[d], device_id_type=MESH
        )
        copy.start()
        to_z.append(copy)
    total = s32[mode] + crecv[z].astype(F32)

    tabt[...] = table((XL, C), True)
    lane = lax.broadcasted_iota(jnp.int32, (8, C), 1) % 8
    own = (lane == lax.broadcasted_iota(jnp.int32, (8, C), 0)).astype(F32)

    @pl.loop(0, XL // 8)
    def _(i):
        rows = tabt[pl.ds(pl.multiple_of(i * 8, 8), 8), :]
        spread = [own * rows[r : r + 1, :] for r in range(8)]
        inv[pl.ds(pl.multiple_of(i * 64, 64), 64), :] = jnp.concatenate(spread, 0).astype(BF)

    @pl.when(jnp.logical_not(has_prev))
    def _():
        fv[0] = jnp.zeros((XL, Z, C), BF)

    @pl.when(jnp.logical_not(has_next))
    def _():
        fv[YL + 1] = jnp.zeros((XL, Z, C), BF)

    for load in others:
        load.wait()
    for copy in to_z:
        copy.wait()
    for d in range(7):
        total = total + zrecv[d].astype(F32)

    ysend[...] = total.astype(BF)
    to_y = pltpu.make_async_remote_copy(ysend, yrecv, ys, yr, device_id=y_peer, device_id_type=MESH)
    to_y.start()
    to_y.wait()
    send_halo(EARLY, NCH)
    total = ysend[...].astype(F32) + yrecv[...].astype(F32)

    real = total[:, 0:8].reshape(YL * Z, C)
    imag = total[:, 8:16].reshape(YL * Z, C)
    both = jnp.concatenate([real, imag], 0).astype(BF)
    by_real = jnp.dot(both, wmix[0], preferred_element_type=F32)
    by_imag = jnp.dot(both, wmix[1], preferred_element_type=F32)
    n = YL * Z
    mixed_real = (by_real[:n] - by_imag[n:]).reshape(YL, 8, C)
    mixed_imag = (by_imag[:n] + by_real[n:]).reshape(YL, 8, C)
    result = jnp.concatenate([mixed_real, mixed_imag], 1).astype(BF)
    mixed[...] = result
    mg[:, mode] = result

    def to_all(d):
        return pltpu.make_async_remote_copy(
            mixed, mg.at[:, mode], gs.at[d], gr.at[d], device_id=z_peer[d], device_id_type=MESH
        )

    def from_z(d):
        zo = (z + 7 - d) % 8
        return pltpu.make_async_remote_copy(
            mixed, mg.at[:, core * 8 + zo], gs.at[d], gr.at[d], device_id=z_peer[d], device_id_type=MESH
        )

    def forward(src, slot, i):
        return pltpu.make_async_remote_copy(
            src, mg.at[:, slot], ks.at[i], kr.at[i], device_id=core_peer, device_id_type=MESH
        )

    arrive = [0, 6, 1, 5, 2, 4, 3]
    for d in order:
        to_all(d).start()
    relay_halo(0, 4)
    first = forward(mixed, mode, 7)
    first.start()
    relays = [first]
    for d in arrive:
        from_z(d).wait_recv()
        slot = core * 8 + (z + 7 - d) % 8
        relay = forward(mg.at[:, slot], slot, d)
        relay.start()
        relays.append(relay)
    for d in order:
        to_all(d).wait_send()
    for relay in relays:
        relay.wait()

    def joined_of(y, x0, cells):
        n = cells * Z
        rows = pl.ds(pl.multiple_of(x0 * Z, n), n)
        at = pl.ds(x0, cells)
        value = jnp.dot(inv[rows, :], mg[y].reshape(C, C), preferred_element_type=F32)
        near = [fv[y + i, at].reshape(n, C).astype(F32) for i in range(3)]
        conv = taps[0:1] * near[0] + taps[1:2] * near[1] + taps[2:3] * near[2]
        return (value + conv).astype(BF), near[1]

    def inner_row(y):
        @pl.loop(0, XL // XB)
        def _(i):
            x0 = pl.multiple_of(i * XB, XB)
            joined, center = joined_of(y, x0, XB)
            ov[pl.ds(x0, XB), y] = mlp(joined, center, w1, b1, w2, b2).astype(BF).reshape(XB, Z, C)

    inner_row(1)
    relay_halo(4, 8)
    inner_row(2)
    inner = pltpu.make_async_copy(ov.at[:, 1:3], out.at[:, 1:3], osem.at[0])
    inner.start()
    relay_halo(8, RELAY)

    def outer(x0, cells):
        @pl.loop(x0 // CROWS, (x0 + cells) // CROWS)
        def _(c):
            send_same(c).wait()

            @pl.when(has_diff)
            def _():
                send_diff(c).wait()

        low, low_center = joined_of(0, x0, cells)
        high_, high_center = joined_of(YL - 1, x0, cells)
        return jnp.concatenate([low, high_], 0), jnp.concatenate([low_center, high_center], 0)

    def store(x0, cells, row, k):
        rows = pl.ds(x0, cells)
        return pltpu.make_async_copy(ov.at[rows, row], out.at[rows, row], osem.at[k])

    def outer_block(x0, cells, k):
        joined, center = outer(x0, cells)
        value = mlp(joined, center, w1, b1, w2, b2).astype(BF)
        rows = pl.ds(x0, cells)
        ov[rows, 0] = value[: cells * Z].reshape(cells, Z, C)
        ov[rows, YL - 1] = value[cells * Z :].reshape(cells, Z, C)
        store(x0, cells, 0, k).start()
        store(x0, cells, YL - 1, k + 1).start()

    wide = LAST // HB

    @pl.loop(0, wide)
    def _(i):
        outer_block(pl.multiple_of(i * HB, HB), HB, 1 + 2 * i)

    outer_block(wide * HB, LAST - wide * HB, 1 + 2 * wide)

    jv[...] = outer(LAST, TB)[0]
    final = pltpu.make_async_copy(jv, last, osem.at[0])
    inner.wait()
    final.start()

    @pl.loop(0, RELAY)
    def _(c):
        @pl.when(c < passed_on)
        def _():
            pass_on(c).wait_send()

    for i in range(wide):
        store(i * HB, HB, 0, 1 + 2 * i).wait()
        store(i * HB, HB, YL - 1, 2 + 2 * i).wait()
    store(wide * HB, LAST - wide * HB, 0, 1 + 2 * wide).wait()
    store(wide * HB, LAST - wide * HB, YL - 1, 2 + 2 * wide).wait()
    final.wait()


def tail(part, f_hbm, joined_hbm, w1, b1, w2, b2, out, ov, fv, jv, isem, osem, jsem, fsem):
    get_joined = pltpu.make_async_copy(joined_hbm, jv, jsem)
    get_joined.start()
    centers = [pltpu.make_async_copy(f_hbm.at[LAST:, (YL - 1) * i], fv.at[i], fsem.at[i]) for i in range(2)]
    for copy in centers:
        copy.start()
    cuts = [*range(0, LAST, HB), LAST, XL]
    pieces = [slice(low, high) for low, high in zip(cuts, cuts[1:])]
    n = len(pieces)
    get = [pltpu.make_async_copy(part.at[p], ov.at[p], isem.at[i]) for i, p in enumerate(pieces[:-1])]
    get.append(pltpu.make_async_copy(part.at[LAST:, 1:3], ov.at[LAST:, 1:3], isem.at[n - 1]))
    put = [pltpu.make_async_copy(ov.at[p], out.at[p], osem.at[i]) for i, p in enumerate(pieces)]
    for copy in get:
        copy.start()
    for i in range(n - 1):
        get[i].wait()
        put[i].start()
    get_joined.wait()
    for copy in centers:
        copy.wait()
    value = mlp(jv[...], fv[...].reshape(2 * TB * Z, C).astype(F32), w1, b1, w2, b2).astype(BF)
    get[n - 1].wait()
    ov[LAST:, 0] = value[: TB * Z].reshape(TB, Z, C)
    ov[LAST:, YL - 1] = value[TB * Z :].reshape(TB, Z, C)
    put[n - 1].start()
    for copy in put:
        copy.wait()


def local(features, spectral_weight, conv_taps, w_in, bias_in, w_out, bias_out):
    dma = pltpu.SemaphoreType.DMA
    vm = pltpu.VMEM
    b1, b2 = bias_in.reshape(1, HID), bias_out.reshape(1, C)
    part, last = pl.pallas_call(
        kernel,
        out_shape=[jax.ShapeDtypeStruct((XL, YL, Z, C), BF), jax.ShapeDtypeStruct((2 * TB * Z, C), BF)],
        in_specs=[pl.BlockSpec(memory_space=pltpu.HBM)] * 7,
        out_specs=[pl.BlockSpec(memory_space=pl.ANY)] * 2,
        scratch_shapes=[
            vm((XL, YL, Z, C), BF),
            vm((2 * TB * Z, C), BF),
            vm((RELAY, CROWS, Z, C), BF),
            vm((YL + 2, XL, Z, C), BF),
            vm((2 * MODES * 8, XL * Z), BF),
            vm((XL * Z, C), BF),
            vm((2 * MODES, XL * Z), F32),
            vm((XL, C), F32),
            vm((MODES, YL, 16, C), F32),
            vm((8, YL, 16, C), BF),
            vm((8, YL, 16, C), BF),
            vm((7, YL, 16, C), BF),
            vm((7, YL, 16, C), BF),
            vm((YL, 16, C), BF),
            vm((YL, 16, C), BF),
            vm((2, C, C), BF),
            vm((YL, 16, C), BF),
            vm((YL, MODES, 16, C), BF),
            vm((3, C), F32),
            vm((C, HID), BF),
            vm((1, HID), F32),
            vm((HID, C), BF),
            vm((1, C), F32),
            dma((YL,)),
            dma((6,)),
            dma((2, NCH)),
            dma((2, NCH)),
            dma,
            dma,
            dma((7,)),
            dma((7,)),
            dma,
            dma,
            dma((7,)),
            dma((7,)),
            dma((8,)),
            dma((8,)),
            dma((RELAY,)),
            dma((RELAY,)),
            dma((9,)),
        ],
        compiler_params=pltpu.CompilerParams(
            collective_id=0, has_side_effects=True, vmem_limit_bytes=36 << 20
        ),
        name="layer",
    )(*[pltpu.with_memory_space_constraint(a, pltpu.HBM) for a in (features, spectral_weight, conv_taps, w_in, b1, w_out, b2)])
    whole = pl.BlockSpec(memory_space=pltpu.VMEM)
    hbm = pl.BlockSpec(memory_space=pl.ANY)
    return pl.pallas_call(
        tail,
        out_shape=jax.ShapeDtypeStruct((XL, YL, Z, C), BF),
        in_specs=[hbm, pl.BlockSpec(memory_space=pltpu.HBM), hbm] + [whole] * 4,
        out_specs=hbm,
        scratch_shapes=[
            vm((XL, YL, Z, C), BF),
            vm((2, TB, Z, C), BF),
            vm((2 * TB * Z, C), BF),
            dma((XL // HB + 1,)),
            dma((XL // HB + 1,)),
            dma,
            dma((2,)),
        ],
        compiler_params=pltpu.CompilerParams(vmem_limit_bytes=24 << 20),
        name="tail",
    )(part, pltpu.with_memory_space_constraint(features, pltpu.HBM), last, w_in, b1, w_out, b2)


def solution(mesh):
    return jax.shard_map(
        local,
        mesh=mesh,
        in_specs=(P("gx", "gy", None, None), P(), P(), P(), P(), P(), P()),
        out_specs=P("gx", "gy", None, None),
        check_vma=False,
    )
```

```python
import functools
import math

import jax
import jax.numpy as jnp
from jax import lax
from jax.experimental import pallas as pl
from jax.experimental.pallas import tpu as pltpu
from jax.sharding import PartitionSpec as P

MESH = pl.DeviceIdType.MESH
BF = jnp.bfloat16
F32 = jnp.float32
X = 8192
MODES = 16
XL = 256
YL = 4
Z = 8
C = 256
HID = 1024
NCH = 16
EARLY = 5
AHEAD = 2
CROWS = XL // NCH
XB = 128
HB = 64
RELAY = 12
TB = 16
LAST = XL - TB
HC = 256


def table(shape, lane_is_mode):
    rows = lax.broadcasted_iota(jnp.int32, shape, 0)
    cols = lax.broadcasted_iota(jnp.int32, shape, 1)
    first = lax.axis_index("gx") * XL
    if lane_is_mode:
        mode, part, x = cols // 16, (cols // 8) % 2, first + rows
    else:
        mode, part, x = rows // 2, rows % 2, first + cols // 8
    turn = (mode * x + part * (X // 4)) % X
    value = jnp.cos((2.0 * math.pi / X) * turn.astype(F32)) * (1.0 / math.sqrt(X))
    if lane_is_mode:
        value = value * jnp.where(mode == 0, 1.0, 2.0)
    return value


def gelu_doubled(x):
    c = math.sqrt(2.0 / math.pi)
    t = jnp.tanh(x * (c + (c * 0.044715) * (x * x)))
    return x + x * t


def mlp(joined, center, w1, b1, w2, b2):
    parts = []
    for h in range(0, HID, HC):
        hidden = jnp.dot(joined, w1[:, h : h + HC], preferred_element_type=F32) + b1[:, h : h + HC]
        parts.append(gelu_doubled(hidden).astype(BF))
    value = 0.5 * jnp.dot(jnp.concatenate(parts, 1), w2[...], preferred_element_type=F32) + b2[...]
    return value if center is None else value + center


def kernel(
    f_hbm, sw_hbm, taps_hbm, w1_hbm, b1_hbm, w2_hbm, b2_hbm,
    out, last,
    ov, jv, rl, fv, fwd, inv, tab, tabt, s32, csend, crecv, zsend, zrecv, ysend, yrecv, wmix, mixed, mg, taps, w1, b1, w2, b2,
    fsem, wsem, hs, hr, cs, cr, zs, zr, ys, yr, gs, gr, ks, kr, rr, fs, here, osem,
):
    gx, gy = lax.axis_index("gx"), lax.axis_index("gy")
    core = gx % 2
    z = (gx // 2) % 8
    base = gx - 2 * z
    core_peer = (base + 2 * z + 1 - 2 * core, gy)
    y_peer = ((gx + 16) % 32, gy)
    z_index = [(z + d) % 8 for d in range(1, 8)]
    z_peer = [(base + 2 * i, gy) for i in z_index]
    mode = core * 8 + z
    column, high = gy // 2, gy % 2
    same = gy + 1 - 2 * high
    diff = gy - 1 + 2 * high
    has_next, has_prev = gy < 7, gy > 0
    has_diff = (diff >= 0) & (diff <= 7)
    from_low, from_high = gy > 1, gy < 6
    relay_to = jnp.where(high == 0, gy + 2, gy - 2)
    sent_by_relay = jnp.where(high == 1, 12 - 4 * column, 4 * column)
    passed_on = jnp.where(high == 0, 12 - 4 * column, 4 * column)

    barrier = pltpu.get_barrier_semaphore()
    for peer in [core_peer, y_peer, (gx, same)]:
        pl.semaphore_signal(barrier, inc=1, device_id=peer, device_id_type=MESH)
    for there, peer in ((has_diff, diff), (from_low, gy - 2), (from_high, gy + 2)):

        @pl.when(there)
        def _():
            pl.semaphore_signal(barrier, inc=1, device_id=(gx, peer), device_id_type=MESH)

    for i, peer in zip(z_index, z_peer):

        @pl.when(i > z)
        def _():
            pl.semaphore_signal(barrier, inc=1, device_id=peer, device_id_type=MESH)

    loads = [pltpu.make_async_copy(f_hbm.at[:, y], fv.at[y + 1], fsem.at[y]) for y in range(YL)]
    for load in loads:
        load.start()
    others = [
        pltpu.make_async_copy(sw_hbm.at[mode], wmix, wsem.at[0]),
        pltpu.make_async_copy(w1_hbm, w1, wsem.at[1]),
        pltpu.make_async_copy(w2_hbm, w2, wsem.at[2]),
        pltpu.make_async_copy(b1_hbm, b1, wsem.at[3]),
        pltpu.make_async_copy(b2_hbm, b2, wsem.at[4]),
        pltpu.make_async_copy(taps_hbm, taps, wsem.at[5]),
    ]
    for load in others:
        load.start()

    tab[...] = table((2 * MODES, XL * Z), False)
    lane = lax.broadcasted_iota(jnp.int32, (8, XL * Z), 1) % 8
    own = (lane == lax.broadcasted_iota(jnp.int32, (8, XL * Z), 0)).astype(F32)
    for i in range(MODES):
        pair = [own * tab[2 * i + p : 2 * i + p + 1, :] for p in range(2)]
        fwd[16 * i : 16 * i + 16, :] = jnp.concatenate(pair, 0).astype(BF)

    row_same, slot_same = jnp.where(high == 0, YL - 1, 0), jnp.where(high == 0, 0, YL + 1)
    row_diff, slot_diff = jnp.where(high == 1, YL - 1, 0), jnp.where(high == 1, 0, YL + 1)

    def block_of(c):
        return c // 4 + c // (NCH - 1)

    def send_same(c):
        rows = pl.ds(c * CROWS, CROWS)
        return pltpu.make_async_remote_copy(
            f_hbm.at[rows, row_same], fv.at[slot_same, rows], hs.at[0], hr.at[0, block_of(c)],
            device_id=(gx, same), device_id_type=MESH,
        )

    def send_diff(c):
        rows = pl.ds(c * CROWS, CROWS)
        return pltpu.make_async_remote_copy(
            f_hbm.at[rows, row_diff], fv.at[slot_diff, rows], hs.at[1], hr.at[1, block_of(c)],
            device_id=(gx, diff), device_id_type=MESH,
        )

    def send_relay(c):
        rows = pl.ds(c * CROWS, CROWS)
        return pltpu.make_async_remote_copy(
            f_hbm.at[rows, row_diff], rl.at[c], hs.at[1], rr.at[c // 4],
            device_id=(gx, same), device_id_type=MESH,
        )

    def pass_on(c):
        rows = pl.ds(c * CROWS, CROWS)
        return pltpu.make_async_remote_copy(
            rl.at[c], fv.at[slot_same, rows], fs.at[c // 4], hr.at[1, block_of(c)],
            device_id=(gx, relay_to), device_id_type=MESH,
        )

    def start_diff(c):
        @pl.when(has_diff & (c < sent_by_relay))
        def _():
            send_relay(c).start()

        @pl.when(has_diff & (c >= sent_by_relay))
        def _():
            send_diff(c).start()

    def step_diff(c):
        @pl.when(c < 12)
        def _():
            start_diff(c + c // 3)

        @pl.when((c < 12) & (c % 3 == 2))
        def _():
            start_diff(c + c // 3 + 1)

    def send_halo(first, last):
        @pl.loop(first, last)
        def _(c):
            send_same(c).start()
            step_diff(c)

    def passed(g):
        rows = pl.ds(4 * g, 4)
        return pltpu.make_async_remote_copy(
            rl.at[rows], rl.at[rows], fs.at[g], rr.at[g], device_id=(gx, relay_to), device_id_type=MESH
        )

    def relay_halo(g):
        @pl.when(4 * g < passed_on)
        def _():
            passed(g).wait_recv()

            @pl.loop(4 * g, 4 * g + 4)
            def _(c):
                pass_on(c).start()

    def transform(y):
        loads[y].wait()
        s = jnp.dot(fwd[...], fv[y + 1].reshape(XL * Z, C), preferred_element_type=F32)
        s32[:, y] = s.reshape(MODES, 16, C)

    for y in range(AHEAD):
        transform(y)
    pl.semaphore_wait(barrier, 3 + z + sum(there.astype(jnp.int32) for there in (has_diff, from_low, from_high)))
    for i, peer in zip(z_index, z_peer):

        @pl.when(i < z)
        def _():
            pl.semaphore_signal(here, inc=1, device_id=peer, device_id_type=MESH)

    send_halo(0, EARLY)
    send_same(EARLY).start()
    for y in range(AHEAD, YL):
        transform(y)
    for k in range(8):
        csend[k] = s32[(1 - core) * 8 + k].astype(BF)

    to_core = pltpu.make_async_remote_copy(csend, crecv, cs, cr, device_id=core_peer, device_id_type=MESH)
    to_core.start()
    to_core.wait()


    @pl.when(z < 7)
    def _():
        pl.semaphore_wait(here, 7 - z)

    order = [3, 2, 4, 1, 5, 0, 6]
    for d in order:
        zo = z_index[d]
        zsend[d] = (s32[core * 8 + zo] + crecv[zo].astype(F32)).astype(BF)
        copy = pltpu.make_async_remote_copy(
            zsend.at[d], zrecv.at[d], zs, zr, device_id=z_peer[d], device_id_type=MESH
        )
        copy.start()
    total = s32[mode] + crecv[z].astype(F32)

    tabt[...] = table((XL, C), True)
    lane = lax.broadcasted_iota(jnp.int32, (8, C), 1) % 8
    own = (lane == lax.broadcasted_iota(jnp.int32, (8, C), 0)).astype(F32)

    @pl.loop(0, XL // 8)
    def _(i):
        rows = tabt[pl.ds(pl.multiple_of(i * 8, 8), 8), :]
        spread = [own * rows[r : r + 1, :] for r in range(8)]
        inv[pl.ds(pl.multiple_of(i * 64, 64), 64), :] = jnp.concatenate(spread, 0).astype(BF)

    @pl.when(jnp.logical_not(has_prev))
    def _():
        fv[0] = jnp.zeros((XL, Z, C), BF)

    @pl.when(jnp.logical_not(has_next))
    def _():
        fv[YL + 1] = jnp.zeros((XL, Z, C), BF)

    for load in others:
        load.wait()
    pltpu.make_async_remote_copy(zsend, zrecv, zs, zr, device_id=z_peer[0], device_id_type=MESH).wait()
    for d in range(7):
        total = total + zrecv[d].astype(F32)

    ysend[...] = total.astype(BF)
    to_y = pltpu.make_async_remote_copy(ysend, yrecv, ys, yr, device_id=y_peer, device_id_type=MESH)
    to_y.start()
    to_y.wait()
    step_diff(EARLY)
    send_halo(EARLY + 1, NCH)
    total = ysend[...].astype(F32) + yrecv[...].astype(F32)

    real = total[:, 0:8].reshape(YL * Z, C)
    imag = total[:, 8:16].reshape(YL * Z, C)
    both = jnp.concatenate([real, imag], 0).astype(BF)
    by_real = jnp.dot(both, wmix[0], preferred_element_type=F32)
    by_imag = jnp.dot(both, wmix[1], preferred_element_type=F32)
    n = YL * Z
    mixed_real = (by_real[:n] - by_imag[n:]).reshape(YL, 8, C)
    mixed_imag = (by_imag[:n] + by_real[n:]).reshape(YL, 8, C)
    result = jnp.concatenate([mixed_real, mixed_imag], 1).astype(BF)
    mixed[...] = result
    mg[:, mode] = result

    def to_all(d):
        return pltpu.make_async_remote_copy(
            mixed, mg.at[:, mode], gs, gr.at[d], device_id=z_peer[d], device_id_type=MESH
        )

    def from_z(d):
        zo = (z + 7 - d) % 8
        return pltpu.make_async_remote_copy(
            mixed, mg.at[:, core * 8 + zo], gs, gr.at[d], device_id=z_peer[d], device_id_type=MESH
        )

    def forward(src, slot):
        return pltpu.make_async_remote_copy(
            src, mg.at[:, slot], ks, kr, device_id=core_peer, device_id_type=MESH
        )

    arrive = [0, 6, 1, 5, 2, 4, 3]
    for d in order:
        to_all(d).start()
    relay_halo(0)
    first = forward(mixed, mode)
    first.start()
    for d in arrive:
        from_z(d).wait_recv()
        slot = core * 8 + (z + 7 - d) % 8
        relay = forward(mg.at[:, slot], slot)
        relay.start()
    relay_halo(1)
    pltpu.make_async_remote_copy(zsend, zrecv, gs, zr, device_id=z_peer[0], device_id_type=MESH).wait_send()
    half = mg.at[:, pl.ds(8 - core * 8, 8)]
    pltpu.make_async_remote_copy(half, half, ks, kr, device_id=core_peer, device_id_type=MESH).wait()

    def joined_of(y, x0, cells):
        n = cells * Z
        rows = pl.ds(pl.multiple_of(x0 * Z, n), n)
        at = pl.ds(x0, cells)
        value = jnp.dot(inv[rows, :], mg[y].reshape(C, C), preferred_element_type=F32)
        near = [fv[y + i, at].reshape(n, C).astype(F32) for i in range(3)]
        conv = taps[0:1] * near[0] + taps[1:2] * near[1] + taps[2:3] * near[2]
        return (value + conv).astype(BF), near[1]

    per_row = XL // XB

    @pl.loop(0, 2 * per_row)
    def _(i):
        y = 1 + i // per_row
        x0 = pl.multiple_of((i % per_row) * XB, XB)
        joined, center = joined_of(y, x0, XB)
        ov[pl.ds(x0, XB), y] = mlp(joined, center, w1, b1, w2, b2).astype(BF).reshape(XB, Z, C)

        @pl.when(i == 1)
        def _():
            relay_halo(2)

    inner = pltpu.make_async_copy(ov.at[:, 1:3], out.at[:, 1:3], osem.at[0])
    inner.start()

    def halo_bytes(stream, row, x0, cells, block):
        at = pl.ds(x0, cells)
        return pltpu.make_async_remote_copy(
            f_hbm.at[at, row], fv.at[0, at], hs.at[stream], hr.at[stream, block],
            device_id=(gx, same), device_id_type=MESH,
        )

    def arrived(x0, cells, block):
        halo_bytes(0, row_same, x0, cells, block).wait_recv()

        @pl.when(has_diff)
        def _():
            halo_bytes(1, row_diff, x0, cells, block).wait_recv()

    def outer(x0, cells, block):
        arrived(x0, cells, block)
        low, low_center = joined_of(0, x0, cells)
        high_, high_center = joined_of(YL - 1, x0, cells)
        return jnp.concatenate([low, high_], 0), jnp.concatenate([low_center, high_center], 0)

    def store(x0, cells, i):
        rows, row = pl.ds(x0, cells), (YL - 1) * i
        return pltpu.make_async_copy(ov.at[rows, row], out.at[rows, row], osem.at[1 + i])

    def outer_block(x0, cells, block):
        joined, center = outer(x0, cells, block)
        value = mlp(joined, center, w1, b1, w2, b2).astype(BF)
        rows = pl.ds(x0, cells)
        ov[rows, 0] = value[: cells * Z].reshape(cells, Z, C)
        ov[rows, YL - 1] = value[cells * Z :].reshape(cells, Z, C)
        for i in range(2):
            store(x0, cells, i).start()

    wide = LAST // HB

    @pl.loop(0, wide)
    def _(i):
        outer_block(pl.multiple_of(i * HB, HB), HB, i)

    outer_block(wide * HB, LAST - wide * HB, wide)

    at, n = slice(LAST, XL), TB * Z
    parts = []
    for y, other in ((0, 2), (YL - 1, YL - 1)):
        value = jnp.dot(inv[LAST * Z :, :], mg[y].reshape(C, C), preferred_element_type=F32)
        for slot in (y + 1, other):
            value = value + taps[slot - y : slot - y + 1] * fv[slot, at].reshape(n, C).astype(F32)
        parts.append(value)
    arrived(LAST, TB, wide + 1)
    low_halo = taps[0:1] * fv[0, at].reshape(n, C).astype(F32)
    high_halo = taps[2:3] * fv[YL + 1, at].reshape(n, C).astype(F32)
    jv[:n] = (parts[0] + low_halo).astype(BF)
    jv[n:] = (parts[1] + high_halo).astype(BF)
    final = pltpu.make_async_copy(jv, last, osem.at[3])
    final.start()

    for g in range(RELAY // 4):

        @pl.when(4 * g < passed_on)
        def _():
            passed(g).wait_send()

    halo_bytes(0, row_same, 0, XL, 0).wait_send()

    @pl.when(has_diff)
    def _():
        halo_bytes(1, row_diff, 0, XL, 0).wait_send()

    inner.wait()
    for i in range(2):
        store(0, LAST, i).wait()
    final.wait()


def tail(part, f_hbm, joined, w1, b1, w2, b2, out, fv, rv, osem, fsem):
    rows = (slice(0, LAST), slice(0, YL)), (slice(LAST, XL), slice(1, YL - 1))
    put = [pltpu.make_async_copy(part.at[at], out.at[at], osem.at[i]) for i, at in enumerate(rows)]
    centers = [pltpu.make_async_copy(f_hbm.at[LAST:, (YL - 1) * i], fv.at[i], fsem.at[i]) for i in range(2)]
    for copy in centers + put:
        copy.start()
    value = mlp(joined[...], None, w1, b1, w2, b2)
    for copy in centers:
        copy.wait()
    value = value + fv[...].reshape(2 * TB * Z, C).astype(F32)
    rv[...] = value.astype(BF).reshape(2, TB, Z, C)
    for i in range(2):
        copy = pltpu.make_async_copy(rv.at[i], out.at[LAST:, (YL - 1) * i], osem.at[2 + i])
        copy.start()
        put.append(copy)
    for copy in put:
        copy.wait()


def local(features, spectral_weight, conv_taps, w_in, bias_in, w_out, bias_out):
    dma = pltpu.SemaphoreType.DMA
    vm = pltpu.VMEM
    b1, b2 = bias_in.reshape(1, HID), bias_out.reshape(1, C)
    part, last = pl.pallas_call(
        kernel,
        out_shape=[jax.ShapeDtypeStruct((XL, YL, Z, C), BF), jax.ShapeDtypeStruct((2 * TB * Z, C), BF)],
        in_specs=[pl.BlockSpec(memory_space=pltpu.HBM)] * 7,
        out_specs=[pl.BlockSpec(memory_space=pl.ANY)] * 2,
        scratch_shapes=[
            vm((XL, YL, Z, C), BF),
            vm((2 * TB * Z, C), BF),
            vm((RELAY, CROWS, Z, C), BF),
            vm((YL + 2, XL, Z, C), BF),
            vm((2 * MODES * 8, XL * Z), BF),
            vm((XL * Z, C), BF),
            vm((2 * MODES, XL * Z), F32),
            vm((XL, C), F32),
            vm((MODES, YL, 16, C), F32),
            vm((8, YL, 16, C), BF),
            vm((8, YL, 16, C), BF),
            vm((7, YL, 16, C), BF),
            vm((7, YL, 16, C), BF),
            vm((YL, 16, C), BF),
            vm((YL, 16, C), BF),
            vm((2, C, C), BF),
            vm((YL, 16, C), BF),
            vm((YL, MODES, 16, C), BF),
            vm((3, C), F32),
            vm((C, HID), BF),
            vm((1, HID), F32),
            vm((HID, C), BF),
            vm((1, C), F32),
            dma((YL,)),
            dma((6,)),
            dma((2,)),
            dma((2, XL // HB + 1)),
            dma,
            dma,
            dma,
            dma,
            dma,
            dma,
            dma,
            dma((7,)),
            dma,
            dma,
            dma((RELAY // 4,)),
            dma((RELAY // 4,)),
            pltpu.SemaphoreType.REGULAR,
            dma((4,)),
        ],
        compiler_params=pltpu.CompilerParams(
            collective_id=0, has_side_effects=True, vmem_limit_bytes=36 << 20
        ),
        name="layer",
    )(*[pltpu.with_memory_space_constraint(a, pltpu.HBM) for a in (features, spectral_weight, conv_taps, w_in, b1, w_out, b2)])
    whole = pl.BlockSpec(memory_space=pltpu.VMEM)
    hbm = pl.BlockSpec(memory_space=pl.ANY)
    return pl.pallas_call(
        tail,
        out_shape=jax.ShapeDtypeStruct((XL, YL, Z, C), BF),
        in_specs=[hbm, hbm] + [whole] * 5,
        out_specs=hbm,
        scratch_shapes=[
            vm((2, TB, Z, C), BF),
            vm((2, TB, Z, C), BF),
            dma((4,)),
            dma((2,)),
        ],
        compiler_params=pltpu.CompilerParams(vmem_limit_bytes=24 << 20),
        name="tail",
    )(part, pltpu.with_memory_space_constraint(features, pltpu.HBM), last, w_in, b1, w_out, b2)


def solution(mesh):
    return jax.shard_map(
        local,
        mesh=mesh,
        in_specs=(P("gx", "gy", None, None), P(), P(), P(), P(), P(), P()),
        out_specs=P("gx", "gy", None, None),
        check_vma=False,
    )
```

```python
import functools
import math

import jax
import jax.numpy as jnp
from jax import lax
from jax.experimental import pallas as pl
from jax.experimental.pallas import tpu as pltpu
from jax.sharding import PartitionSpec as P

MESH = pl.DeviceIdType.MESH
BF = jnp.bfloat16
F32 = jnp.float32
X = 8192
MODES = 16
XL = 256
YL = 4
Z = 8
C = 256
HID = 1024
NCH = 16
EARLY = 5
AHEAD = 2
CROWS = XL // NCH
XB = 128
HB = 64
RELAY = 12
TB = 16
LAST = XL - TB
HC = 256


def table(shape, lane_is_mode):
    rows = lax.broadcasted_iota(jnp.int32, shape, 0)
    cols = lax.broadcasted_iota(jnp.int32, shape, 1)
    first = lax.axis_index("gx") * XL
    if lane_is_mode:
        mode, part, x = cols // 16, (cols // 8) % 2, first + rows
    else:
        mode, part, x = rows // 2, rows % 2, first + cols // 8
    turn = (mode * x + part * (X // 4)) % X
    value = jnp.cos((2.0 * math.pi / X) * turn.astype(F32)) * (1.0 / math.sqrt(X))
    if lane_is_mode:
        value = value * jnp.where(mode == 0, 1.0, 2.0)
    return value


def gelu_doubled(x):
    c = math.sqrt(2.0 / math.pi)
    t = jnp.tanh(x * (c + (c * 0.044715) * (x * x)))
    return x + x * t


def mlp(joined, center, w1, b1, w2, b2):
    parts = []
    for h in range(0, HID, HC):
        hidden = jnp.dot(joined, w1[:, h : h + HC], preferred_element_type=F32) + b1[:, h : h + HC]
        parts.append(gelu_doubled(hidden).astype(BF))
    value = 0.5 * jnp.dot(jnp.concatenate(parts, 1), w2[...], preferred_element_type=F32) + b2[...]
    return value if center is None else value + center


def kernel(
    f_hbm, sw_hbm, taps_hbm, w1_hbm, b1_hbm, w2_hbm, b2_hbm,
    out, last,
    ov, jv, rl, fv, fwd, inv, tab, tabt, s32, csend, crecv, zsend, zrecv, ysend, yrecv, wmix, mixed, mg, taps, w1, b1, w2, b2,
    fsem, wsem, hs, hr, cs, cr, zs, zr, ys, yr, gs, gr, ks, kr, rr, fs, here, osem,
):
    gx, gy = lax.axis_index("gx"), lax.axis_index("gy")
    core = gx % 2
    z = (gx // 2) % 8
    base = gx - 2 * z
    core_peer = (base + 2 * z + 1 - 2 * core, gy)
    y_peer = ((gx + 16) % 32, gy)
    z_index = [(z + d) % 8 for d in range(1, 8)]
    z_peer = [(base + 2 * i, gy) for i in z_index]
    mode = core * 8 + z
    column, high = gy // 2, gy % 2
    same = gy + 1 - 2 * high
    diff = gy - 1 + 2 * high
    has_next, has_prev = gy < 7, gy > 0
    has_diff = (diff >= 0) & (diff <= 7)
    from_low, from_high = gy > 1, gy < 6
    relay_to = jnp.where(high == 0, gy + 2, gy - 2)
    sent_by_relay = jnp.where(high == 1, 12 - 4 * column, 4 * column)
    passed_on = jnp.where(high == 0, 12 - 4 * column, 4 * column)

    barrier = pltpu.get_barrier_semaphore()
    for peer in [core_peer, y_peer, (gx, same)]:
        pl.semaphore_signal(barrier, inc=1, device_id=peer, device_id_type=MESH)
    for there, peer in ((has_diff, diff), (from_low, gy - 2), (from_high, gy + 2)):

        @pl.when(there)
        def _():
            pl.semaphore_signal(barrier, inc=1, device_id=(gx, peer), device_id_type=MESH)

    for i, peer in zip(z_index, z_peer):

        @pl.when(i > z)
        def _():
            pl.semaphore_signal(barrier, inc=1, device_id=peer, device_id_type=MESH)

    loads = [pltpu.make_async_copy(f_hbm.at[:, y], fv.at[y + 1], fsem.at[y]) for y in range(YL)]
    for load in loads:
        load.start()
    others = [
        pltpu.make_async_copy(sw_hbm.at[mode], wmix, wsem.at[0]),
        pltpu.make_async_copy(w1_hbm, w1, wsem.at[1]),
        pltpu.make_async_copy(w2_hbm, w2, wsem.at[2]),
        pltpu.make_async_copy(b1_hbm, b1, wsem.at[3]),
        pltpu.make_async_copy(b2_hbm, b2, wsem.at[4]),
        pltpu.make_async_copy(taps_hbm, taps, wsem.at[5]),
    ]
    for load in others:
        load.start()

    tab[...] = table((2 * MODES, XL * Z), False)
    lane = lax.broadcasted_iota(jnp.int32, (8, XL * Z), 1) % 8
    own = (lane == lax.broadcasted_iota(jnp.int32, (8, XL * Z), 0)).astype(F32)
    for i in range(MODES):
        pair = [own * tab[2 * i + p : 2 * i + p + 1, :] for p in range(2)]
        fwd[16 * i : 16 * i + 16, :] = jnp.concatenate(pair, 0).astype(BF)

    row_same, slot_same = jnp.where(high == 0, YL - 1, 0), jnp.where(high == 0, 0, YL + 1)
    row_diff, slot_diff = jnp.where(high == 1, YL - 1, 0), jnp.where(high == 1, 0, YL + 1)

    def block_of(c):
        return c // 4 + c // (NCH - 1)

    def send_same(c):
        rows = pl.ds(c * CROWS, CROWS)
        return pltpu.make_async_remote_copy(
            f_hbm.at[rows, row_same], fv.at[slot_same, rows], hs.at[0], hr.at[0, block_of(c)],
            device_id=(gx, same), device_id_type=MESH,
        )

    def send_diff(c):
        rows = pl.ds(c * CROWS, CROWS)
        return pltpu.make_async_remote_copy(
            f_hbm.at[rows, row_diff], fv.at[slot_diff, rows], hs.at[1], hr.at[1, block_of(c)],
            device_id=(gx, diff), device_id_type=MESH,
        )

    def send_relay(c):
        rows = pl.ds(c * CROWS, CROWS)
        return pltpu.make_async_remote_copy(
            f_hbm.at[rows, row_diff], rl.at[c], hs.at[1], rr.at[c // 4],
            device_id=(gx, same), device_id_type=MESH,
        )

    def pass_on(c):
        rows = pl.ds(c * CROWS, CROWS)
        return pltpu.make_async_remote_copy(
            rl.at[c], fv.at[slot_same, rows], fs.at[c // 4], hr.at[1, block_of(c)],
            device_id=(gx, relay_to), device_id_type=MESH,
        )

    def start_diff(c):
        @pl.when(has_diff & (c < sent_by_relay))
        def _():
            send_relay(c).start()

        @pl.when(has_diff & (c >= sent_by_relay))
        def _():
            send_diff(c).start()

    def step_diff(c):
        @pl.when(c < 12)
        def _():
            start_diff(c + c // 3)

        @pl.when((c < 12) & (c % 3 == 2))
        def _():
            start_diff(c + c // 3 + 1)

    def send_halo(first, last):
        @pl.loop(first, last)
        def _(c):
            send_same(c).start()
            step_diff(c)

    def passed(g):
        rows = pl.ds(4 * g, 4)
        return pltpu.make_async_remote_copy(
            rl.at[rows], rl.at[rows], fs.at[g], rr.at[g], device_id=(gx, relay_to), device_id_type=MESH
        )

    def relay_halo(g):
        @pl.when(4 * g < passed_on)
        def _():
            passed(g).wait_recv()

            @pl.loop(4 * g, 4 * g + 4)
            def _(c):
                pass_on(c).start()

    def transform(y):
        loads[y].wait()
        s = jnp.dot(fwd[...], fv[y + 1].reshape(XL * Z, C), preferred_element_type=F32)
        s32[:, y] = s.reshape(MODES, 16, C)

    for y in range(AHEAD):
        transform(y)
    pl.semaphore_wait(barrier, 3 + z + sum(there.astype(jnp.int32) for there in (has_diff, from_low, from_high)))
    for i, peer in zip(z_index, z_peer):

        @pl.when(i < z)
        def _():
            pl.semaphore_signal(here, inc=1, device_id=peer, device_id_type=MESH)

    send_halo(0, EARLY)
    send_same(EARLY).start()
    start_diff(EARLY + EARLY // 3)
    for y in range(AHEAD, YL):
        transform(y)
    for k in range(8):
        csend[k] = s32[(1 - core) * 8 + k].astype(BF)

    to_core = pltpu.make_async_remote_copy(csend, crecv, cs, cr, device_id=core_peer, device_id_type=MESH)
    to_core.start()
    to_core.wait()


    @pl.when(z < 7)
    def _():
        pl.semaphore_wait(here, 7 - z)

    order = [3, 2, 4, 1, 5, 0, 6]
    for d in order:
        zo = z_index[d]
        zsend[d] = (s32[core * 8 + zo] + crecv[zo].astype(F32)).astype(BF)
        copy = pltpu.make_async_remote_copy(
            zsend.at[d], zrecv.at[d], zs, zr, device_id=z_peer[d], device_id_type=MESH
        )
        copy.start()
    total = s32[mode] + crecv[z].astype(F32)

    tabt[...] = table((XL, C), True)
    lane = lax.broadcasted_iota(jnp.int32, (8, C), 1) % 8
    own = (lane == lax.broadcasted_iota(jnp.int32, (8, C), 0)).astype(F32)

    @pl.loop(0, XL // 8)
    def _(i):
        rows = tabt[pl.ds(pl.multiple_of(i * 8, 8), 8), :]
        spread = [own * rows[r : r + 1, :] for r in range(8)]
        inv[pl.ds(pl.multiple_of(i * 64, 64), 64), :] = jnp.concatenate(spread, 0).astype(BF)

    @pl.when(jnp.logical_not(has_prev))
    def _():
        fv[0] = jnp.zeros((XL, Z, C), BF)

    @pl.when(jnp.logical_not(has_next))
    def _():
        fv[YL + 1] = jnp.zeros((XL, Z, C), BF)

    for load in others:
        load.wait()
    pltpu.make_async_remote_copy(zsend, zrecv, zs, zr, device_id=z_peer[0], device_id_type=MESH).wait()
    for d in range(7):
        total = total + zrecv[d].astype(F32)

    ysend[...] = total.astype(BF)
    to_y = pltpu.make_async_remote_copy(ysend, yrecv, ys, yr, device_id=y_peer, device_id_type=MESH)
    to_y.start()
    to_y.wait()
    start_diff(EARLY + EARLY // 3 + 1)
    send_halo(EARLY + 1, NCH)
    total = ysend[...].astype(F32) + yrecv[...].astype(F32)

    real = total[:, 0:8].reshape(YL * Z, C)
    imag = total[:, 8:16].reshape(YL * Z, C)
    both = jnp.concatenate([real, imag], 0).astype(BF)
    by_real = jnp.dot(both, wmix[0], preferred_element_type=F32)
    by_imag = jnp.dot(both, wmix[1], preferred_element_type=F32)
    n = YL * Z
    mixed_real = (by_real[:n] - by_imag[n:]).reshape(YL, 8, C)
    mixed_imag = (by_imag[:n] + by_real[n:]).reshape(YL, 8, C)
    result = jnp.concatenate([mixed_real, mixed_imag], 1).astype(BF)
    mixed[...] = result
    mg[:, mode] = result

    def to_all(d):
        return pltpu.make_async_remote_copy(
            mixed, mg.at[:, mode], gs, gr.at[d], device_id=z_peer[d], device_id_type=MESH
        )

    def from_z(d):
        zo = (z + 7 - d) % 8
        return pltpu.make_async_remote_copy(
            mixed, mg.at[:, core * 8 + zo], gs, gr.at[d], device_id=z_peer[d], device_id_type=MESH
        )

    def forward(src, slot):
        return pltpu.make_async_remote_copy(
            src, mg.at[:, slot], ks, kr, device_id=core_peer, device_id_type=MESH
        )

    arrive = [0, 6, 1, 5, 2, 4, 3]
    for d in order:
        to_all(d).start()
    relay_halo(0)
    first = forward(mixed, mode)
    first.start()
    for d in arrive:
        from_z(d).wait_recv()
        slot = core * 8 + (z + 7 - d) % 8
        relay = forward(mg.at[:, slot], slot)
        relay.start()
    relay_halo(1)
    pltpu.make_async_remote_copy(zsend, zrecv, gs, zr, device_id=z_peer[0], device_id_type=MESH).wait_send()
    half = mg.at[:, pl.ds(8 - core * 8, 8)]
    pltpu.make_async_remote_copy(half, half, ks, kr, device_id=core_peer, device_id_type=MESH).wait()

    def joined_of(y, x0, cells):
        n = cells * Z
        rows = pl.ds(pl.multiple_of(x0 * Z, n), n)
        at = pl.ds(x0, cells)
        value = jnp.dot(inv[rows, :], mg[y].reshape(C, C), preferred_element_type=F32)
        near = [fv[y + i, at].reshape(n, C).astype(F32) for i in range(3)]
        conv = taps[0:1] * near[0] + taps[1:2] * near[1] + taps[2:3] * near[2]
        return (value + conv).astype(BF), near[1]

    per_row = XL // XB

    @pl.loop(0, 2 * per_row)
    def _(i):
        y = 1 + i // per_row
        x0 = pl.multiple_of((i % per_row) * XB, XB)
        joined, center = joined_of(y, x0, XB)
        ov[pl.ds(x0, XB), y] = mlp(joined, center, w1, b1, w2, b2).astype(BF).reshape(XB, Z, C)

        @pl.when(i == 1)
        def _():
            relay_halo(2)

    inner = pltpu.make_async_copy(ov.at[:, 1:3], out.at[:, 1:3], osem.at[0])
    inner.start()

    def halo_bytes(stream, row, x0, cells, block):
        at = pl.ds(x0, cells)
        return pltpu.make_async_remote_copy(
            f_hbm.at[at, row], fv.at[0, at], hs.at[stream], hr.at[stream, block],
            device_id=(gx, same), device_id_type=MESH,
        )

    def arrived(x0, cells, block):
        halo_bytes(0, row_same, x0, cells, block).wait_recv()

        @pl.when(has_diff)
        def _():
            halo_bytes(1, row_diff, x0, cells, block).wait_recv()

    def outer(x0, cells, block):
        arrived(x0, cells, block)
        low, low_center = joined_of(0, x0, cells)
        high_, high_center = joined_of(YL - 1, x0, cells)
        return jnp.concatenate([low, high_], 0), jnp.concatenate([low_center, high_center], 0)

    def store(x0, cells, i):
        rows, row = pl.ds(x0, cells), (YL - 1) * i
        return pltpu.make_async_copy(ov.at[rows, row], out.at[rows, row], osem.at[1 + i])

    def outer_block(x0, cells, block):
        joined, center = outer(x0, cells, block)
        value = mlp(joined, center, w1, b1, w2, b2).astype(BF)
        rows = pl.ds(x0, cells)
        ov[rows, 0] = value[: cells * Z].reshape(cells, Z, C)
        ov[rows, YL - 1] = value[cells * Z :].reshape(cells, Z, C)
        for i in range(2):
            store(x0, cells, i).start()

    wide = LAST // HB

    @pl.loop(0, wide)
    def _(i):
        outer_block(pl.multiple_of(i * HB, HB), HB, i)

    outer_block(wide * HB, LAST - wide * HB, wide)

    at, n = slice(LAST, XL), TB * Z
    parts = []
    for y, other in ((0, 2), (YL - 1, YL - 1)):
        value = jnp.dot(inv[LAST * Z :, :], mg[y].reshape(C, C), preferred_element_type=F32)
        for slot in (y + 1, other):
            value = value + taps[slot - y : slot - y + 1] * fv[slot, at].reshape(n, C).astype(F32)
        parts.append(value)
    arrived(LAST, TB, wide + 1)
    low_halo = taps[0:1] * fv[0, at].reshape(n, C).astype(F32)
    high_halo = taps[2:3] * fv[YL + 1, at].reshape(n, C).astype(F32)
    jv[:n] = (parts[0] + low_halo).astype(BF)
    jv[n:] = (parts[1] + high_halo).astype(BF)
    final = pltpu.make_async_copy(jv, last, osem.at[3])
    final.start()

    for g in range(RELAY // 4):

        @pl.when(4 * g < passed_on)
        def _():
            passed(g).wait_send()

    halo_bytes(0, row_same, 0, XL, 0).wait_send()

    @pl.when(has_diff)
    def _():
        halo_bytes(1, row_diff, 0, XL, 0).wait_send()

    inner.wait()
    for i in range(2):
        store(0, LAST, i).wait()
    final.wait()


def tail(part, f_hbm, joined, w1, b1, w2, b2, out, fv, rv, osem, fsem):
    rows = (slice(0, LAST), slice(0, YL)), (slice(LAST, XL), slice(1, YL - 1))
    put = [pltpu.make_async_copy(part.at[at], out.at[at], osem.at[i]) for i, at in enumerate(rows)]
    centers = [pltpu.make_async_copy(f_hbm.at[LAST:, (YL - 1) * i], fv.at[i], fsem.at[i]) for i in range(2)]
    for copy in centers + put:
        copy.start()
    value = mlp(joined[...], None, w1, b1, w2, b2)
    for copy in centers:
        copy.wait()
    value = value + fv[...].reshape(2 * TB * Z, C).astype(F32)
    rv[...] = value.astype(BF).reshape(2, TB, Z, C)
    for i in range(2):
        copy = pltpu.make_async_copy(rv.at[i], out.at[LAST:, (YL - 1) * i], osem.at[2 + i])
        copy.start()
        put.append(copy)
    for copy in put:
        copy.wait()


def local(features, spectral_weight, conv_taps, w_in, bias_in, w_out, bias_out):
    dma = pltpu.SemaphoreType.DMA
    vm = pltpu.VMEM
    b1, b2 = bias_in.reshape(1, HID), bias_out.reshape(1, C)
    part, last = pl.pallas_call(
        kernel,
        out_shape=[jax.ShapeDtypeStruct((XL, YL, Z, C), BF), jax.ShapeDtypeStruct((2 * TB * Z, C), BF)],
        in_specs=[pl.BlockSpec(memory_space=pltpu.HBM)] * 7,
        out_specs=[pl.BlockSpec(memory_space=pl.ANY)] * 2,
        scratch_shapes=[
            vm((XL, YL, Z, C), BF),
            vm((2 * TB * Z, C), BF),
            vm((RELAY, CROWS, Z, C), BF),
            vm((YL + 2, XL, Z, C), BF),
            vm((2 * MODES * 8, XL * Z), BF),
            vm((XL * Z, C), BF),
            vm((2 * MODES, XL * Z), F32),
            vm((XL, C), F32),
            vm((MODES, YL, 16, C), F32),
            vm((8, YL, 16, C), BF),
            vm((8, YL, 16, C), BF),
            vm((7, YL, 16, C), BF),
            vm((7, YL, 16, C), BF),
            vm((YL, 16, C), BF),
            vm((YL, 16, C), BF),
            vm((2, C, C), BF),
            vm((YL, 16, C), BF),
            vm((YL, MODES, 16, C), BF),
            vm((3, C), F32),
            vm((C, HID), BF),
            vm((1, HID), F32),
            vm((HID, C), BF),
            vm((1, C), F32),
            dma((YL,)),
            dma((6,)),
            dma((2,)),
            dma((2, XL // HB + 1)),
            dma,
            dma,
            dma,
            dma,
            dma,
            dma,
            dma,
            dma((7,)),
            dma,
            dma,
            dma((RELAY // 4,)),
            dma((RELAY // 4,)),
            pltpu.SemaphoreType.REGULAR,
            dma((4,)),
        ],
        compiler_params=pltpu.CompilerParams(
            collective_id=0, has_side_effects=True, vmem_limit_bytes=36 << 20
        ),
        name="layer",
    )(*[pltpu.with_memory_space_constraint(a, pltpu.HBM) for a in (features, spectral_weight, conv_taps, w_in, b1, w_out, b2)])
    whole = pl.BlockSpec(memory_space=pltpu.VMEM)
    hbm = pl.BlockSpec(memory_space=pl.ANY)
    return pl.pallas_call(
        tail,
        out_shape=jax.ShapeDtypeStruct((XL, YL, Z, C), BF),
        in_specs=[hbm, hbm] + [whole] * 5,
        out_specs=hbm,
        scratch_shapes=[
            vm((2, TB, Z, C), BF),
            vm((2, TB, Z, C), BF),
            dma((4,)),
            dma((2,)),
        ],
        compiler_params=pltpu.CompilerParams(vmem_limit_bytes=24 << 20),
        name="tail",
    )(part, pltpu.with_memory_space_constraint(features, pltpu.HBM), last, w_in, b1, w_out, b2)


def solution(mesh):
    return jax.shard_map(
        local,
        mesh=mesh,
        in_specs=(P("gx", "gy", None, None), P(), P(), P(), P(), P(), P()),
        out_specs=P("gx", "gy", None, None),
        check_vma=False,
    )
```
